32 devices in a mesh: grp: 4 (over x, core), dp: 8 (over z, y).
Axes of the slice: x: 2, y: 2, z: 4, core: 2. Of those that a mesh axis runs over, the one named last changes fastest.
Arguments:
- inputs: bfloat16 [32, 256, 768], P(('grp', 'dp')), may hold values from -36 to 36
- segment_ids: int32 [32, 256], P(('grp', 'dp')), may hold values from 0 to 4, never falling along the last dimension, each value on 1 to 128 neighbouring positions
- out_grad: bfloat16 [32, 256, 768], P(('grp', 'dp')), may hold values from -6 to 6
- norm_gain: float32 [768], P('grp'), may hold values from 0.4 to 4, as said below
- in_weight: float32 [768, 3352], P('grp'), may hold values from -0.21875 to 0.21875
- conv_params: float32 [5, 1792], P(None, 'grp'), may hold values from -3 to 3
- head_params: float32 [3, 24], P(None, 'grp'), may hold values from -7 to 2.8
- gate_gain: float32 [1536], P('grp'), may hold values from 0.4 to 4, as said below
- out_weight: float32 [1536, 768], P('grp'), may hold values from -0.15625 to 0.15625
- norm_gain_moments: float32 [2, 768], P(None, 'grp'), may hold values from -0.12 to 0.12, as said below
- in_weight_moments: float32 [2, 768, 3352], P(None, 'grp'), may hold values from -0.015 to 0.015, as said below
- conv_params_moments: float32 [2, 5, 1792], P(None, None, 'grp'), may hold values from -0.045 to 0.045, as said below
- head_params_moments: float32 [2, 3, 24], P(None, None, 'grp'), may hold values from -0.06 to 0.06, as said below
- gate_gain_moments: float32 [2, 1536], P(None, 'grp'), may hold values from -0.045 to 0.045, as said below
- out_weight_moments: float32 [2, 1536, 768], P(None, 'grp'), may hold values from -0.015 to 0.015, as said below
Outputs:
- block_out: bfloat16 [32, 256, 768], P(('grp', 'dp'))
- input_grad: float32 [32, 256, 768], P(('grp', 'dp'))
- norm_gain_grad: float32 [768], P('grp')
- in_weight_grad: float32 [768, 3352], P('grp')
- conv_params_grad: float32 [5, 1792], P(None, 'grp')
- head_params_grad: float32 [3, 24], P(None, 'grp')
- gate_gain_grad: float32 [1536], P('grp')
- out_weight_grad: float32 [1536, 768], P('grp')
- new_norm_gain: float32 [768], P('grp')
- new_in_weight: float32 [768, 3352], P('grp')
- new_conv_params: float32 [5, 1792], P(None, 'grp')
- new_head_params: float32 [3, 24], P(None, 'grp')
- new_gate_gain: float32 [1536], P('grp')
- new_out_weight: float32 [1536, 768], P('grp')
- new_norm_gain_moments: float32 [2, 768], P(None, 'grp')
- new_in_weight_moments: float32 [2, 768, 3352], P(None, 'grp')
- new_conv_params_moments: float32 [2, 5, 1792], P(None, None, 'grp')
- new_head_params_moments: float32 [2, 3, 24], P(None, None, 'grp')
- new_gate_gain_moments: float32 [2, 1536], P(None, 'grp')
- new_out_weight_moments: float32 [2, 1536, 768], P(None, 'grp')
The draws below stay inside these ranges and needn't reach their ends.
Inputs may be any that keep to these rules, and one draw needn't show every extreme that they name: `segment_ids`: within each sequence the ids never fall, and no document spans more than 128 positions. `norm_gain`: every entry is positive. `gate_gain`: every entry is positive. `norm_gain_moments`: every entry of row 1 is positive. `in_weight_moments`: every entry of row 1 is positive. `conv_params_moments`: every entry of row 1 is positive. `head_params_moments`: every entry of row 1 is positive. `gate_gain_moments`: every entry of row 1 is positive. `out_weight_moments`: every entry of row 1 is positive.
All inputs are finite; a program needn't handle non-finite values.
Results may differ from the reference program's by a relative error of at most 0.0014.
The reference program's roundings to bfloat16 on the way count: a program that leaves them out, or rounds other values in their place, can miss the bound.
Values may be sent and summed in bfloat16 or wider, within the bound.
A program may use at most 128 MiB of HBM per device.

```python
import math
import jax
import jax.numpy as jnp
import numpy as np
from jax import lax

D = 768
HEADS = 24
KW = 4
STRETCH = 256
SEQ_LEN = 256
STEP = 5
DI = 1536
CONV = 1792
NPROJ = 3352
SEQS = 32


def moment_pair(key, shape, factor):
    total_params = D + D * NPROJ + (KW + 1) * CONV + 3 * HEADS + DI + DI * D
    scale_val = factor / math.sqrt(total_params)
    first_key = jax.random.fold_in(key, 11)
    second_key = jax.random.fold_in(key, 12)
    first = 0.3 * scale_val * jax.random.truncated_normal(first_key, -4.0, 4.0, shape, jnp.float32)
    second = 0.004 * scale_val * scale_val * jnp.exp(jax.random.uniform(second_key, shape, jnp.float32, math.log(0.3), math.log(3.0)))
    return jnp.stack([first, jnp.sqrt(second)])


def ramp_gain(key, count):
    rise = 3.0
    ramp = rise ** (jnp.arange(count, dtype=jnp.float32) / (count - 1))
    rough = jax.random.uniform(jax.random.fold_in(key, 21), (count,), jnp.float32, 0.7, 1.3)
    return 0.6 * ramp * rough


def draw_inputs(key, part):
    base_key = jax.random.fold_in(key, 31)
    row_key = jax.random.fold_in(key, 32)
    col_key = jax.random.fold_in(key, 33)
    shape = (SEQS, SEQ_LEN, D)
    base = jax.random.truncated_normal(base_key, -4.0, 4.0, shape, jnp.float32)
    row_scale = jnp.exp(jax.random.uniform(row_key, (SEQS, SEQ_LEN, 1), jnp.float32, math.log(0.3), math.log(3.0)))
    col_scale = jnp.exp(jax.random.uniform(col_key, (D,), jnp.float32, math.log(0.3), math.log(3.0)))
    return (base * row_scale * col_scale).astype(jnp.bfloat16)


def draw_norm_gain(key, part):
    return ramp_gain(jax.random.fold_in(key, 41), D)


def draw_gate_gain(key, part):
    return ramp_gain(jax.random.fold_in(key, 42), DI)


def draw_head_params(key, part):
    step_key = jax.random.fold_in(key, 51)
    rate_key = jax.random.fold_in(key, 52)
    skip_key = jax.random.fold_in(key, 53)
    low_step, high_step = (0.001, 0.1)
    step_init = jnp.exp(jax.random.uniform(step_key, (HEADS,), jnp.float32, math.log(low_step), math.log(high_step)))
    step_bias = step_init + jnp.log(-jnp.expm1(-step_init))
    rate_log = jnp.log(jax.random.uniform(rate_key, (HEADS,), jnp.float32, 1.0, 16.0))
    skip_factor = jax.random.uniform(skip_key, (HEADS,), jnp.float32, 0.5, 1.5)
    return jnp.stack([step_bias, rate_log, skip_factor])


def draw_norm_gain_moments(key, part):
    return moment_pair(jax.random.fold_in(key, 61), (D,), 8.0)


def draw_in_weight_moments(key, part):
    return moment_pair(jax.random.fold_in(key, 62), (D, NPROJ), 1.0)


def draw_conv_params_moments(key, part):
    return moment_pair(jax.random.fold_in(key, 63), (KW + 1, CONV), 3.0)


def draw_head_params_moments(key, part):
    return moment_pair(jax.random.fold_in(key, 64), (3, HEADS), 4.0)


def draw_gate_gain_moments(key, part):
    return moment_pair(jax.random.fold_in(key, 65), (DI,), 3.0)


def draw_out_weight_moments(key, part):
    return moment_pair(jax.random.fold_in(key, 66), (DI, D), 1.0)


def steps_of(own_key, shape, shards, least, high):
    gain = 1.0
    for dim, blocks in shards:
        draws = jax.random.uniform(jax.random.fold_in(jax.random.fold_in(own_key, 6), dim), (blocks,), jnp.float32, least / len(shards), high / len(shards))
        gain = gain * jnp.repeat(jnp.exp(draws), shape[dim] // blocks).reshape((-1,) + (1,) * (len(shape) - 1 - dim))
    return gain


def length_profile(number_of, total, limit, skew):
    loads = [(1 << 20) // math.isqrt(grade ** skew) + 1 for grade in range(2, number_of + 1)]
    spare, counts = total - limit - (number_of - 1), [1] * (number_of - 1)
    while spare > 0:
        free = [i for i in range(number_of - 1) if counts[i] < limit]
        pool, left = sum([loads[i] for i in free]), spare
        for i in free:
            addition = min(limit - counts[i], max(1, left * loads[i] // pool), spare)
            counts[i] = counts[i] + addition
            spare = spare - addition
    return np.array([limit] + counts)


def uneven_parts(key, amount, total, limit, skew):
    if amount == 2:
        one = jax.random.randint(key, (), max(1, total - limit), min(limit, total - 1) + 1)
        return jnp.stack([one, total - one])
    sizes = jnp.asarray(length_profile(amount, total, limit, skew), jnp.int32)
    pairs = (amount - 1) // 2
    donor, taker = sizes[1:1 + 2 * pairs:2], sizes[2:2 + 2 * pairs:2]
    slack = jnp.minimum(donor - 1, limit - taker)
    moved = jax.random.randint(jax.random.fold_in(key, 1), (pairs,), 0, 1 << 20) % (slack + 1)
    sizes = sizes.at[1:1 + 2 * pairs:2].set(donor - moved).at[2:2 + 2 * pairs:2].set(taker + moved)
    return sizes[jax.random.permutation(jax.random.fold_in(key, 2), amount)]


def normal_values(key, dims, scale, reach, cuts=(), kind=jnp.bfloat16):
    loudness = steps_of(key, dims, cuts, -0.22, 0.18) if cuts else 1.0
    values = jax.random.normal(key, dims, jnp.float32) * scale * loudness
    return jnp.minimum(jnp.maximum(values, -reach), reach).astype(kind)


def setup_inputs(seed: int = 0) -> dict:
    seeds = jax.random.split(jax.random.key(seed), 16)
    inputs = draw_inputs(jax.random.fold_in(seeds[15], 71), 0)
    segment_ids = jax.vmap(lambda own: jnp.searchsorted(jnp.cumsum(uneven_parts(own, 5, SEQ_LEN, SEQ_LEN // 2, 0)), jnp.arange(SEQ_LEN), side="right"))(jax.random.split(seeds[1], SEQS)).reshape((SEQS, SEQ_LEN)).astype(jnp.int32)
    out_grad = normal_values(seeds[2], (SEQS, SEQ_LEN, D), 1.0, 6.0, ((0, 32),))
    norm_gain = draw_norm_gain(jax.random.fold_in(seeds[15], 71), 0)
    in_weight = normal_values(seeds[4], (D, NPROJ), D ** -0.5, 0.21875, ((0, 4),), jnp.float32)
    conv_params = normal_values(seeds[5], (KW + 1, CONV), KW ** -0.5, 3.0, ((1, 4),), jnp.float32)
    head_params = draw_head_params(jax.random.fold_in(seeds[15], 71), 0)
    gate_gain = draw_gate_gain(jax.random.fold_in(seeds[15], 71), 0)
    out_weight = normal_values(seeds[8], (DI, D), DI ** -0.5, 0.15625, ((0, 4),), jnp.float32)
    norm_gain_moments = draw_norm_gain_moments(jax.random.fold_in(seeds[15], 71), 0)
    in_weight_moments = draw_in_weight_moments(jax.random.fold_in(seeds[15], 71), 0)
    conv_params_moments = draw_conv_params_moments(jax.random.fold_in(seeds[15], 71), 0)
    head_params_moments = draw_head_params_moments(jax.random.fold_in(seeds[15], 71), 0)
    gate_gain_moments = draw_gate_gain_moments(jax.random.fold_in(seeds[15], 71), 0)
    out_weight_moments = draw_out_weight_moments(jax.random.fold_in(seeds[15], 71), 0)
    return dict(inputs=inputs, segment_ids=segment_ids, out_grad=out_grad, norm_gain=norm_gain, in_weight=in_weight, conv_params=conv_params, head_params=head_params, gate_gain=gate_gain, out_weight=out_weight, norm_gain_moments=norm_gain_moments, in_weight_moments=in_weight_moments, conv_params_moments=conv_params_moments, head_params_moments=head_params_moments, gate_gain_moments=gate_gain_moments, out_weight_moments=out_weight_moments)


norm_eps = 1e-05
clip_limit = 1.0
beta_first = 0.9
beta_second = 0.999
adam_eps = 1e-08
learn_rate = 0.02
weight_decay = 0.1

def norm_rows(features, gain_vec):
    inverse = lax.rsqrt(lax.optimization_barrier(jnp.mean(features * features, axis=-1, keepdims=True)) + norm_eps)
    return features * inverse * gain_vec

def scan_blocks(head_vals, step_size, log_rate, write_proj, read_proj, seg_row):
    highest = lax.Precision.HIGHEST
    length, head_count, head_width = head_vals.shape
    blocks = length // STRETCH
    block_vals = head_vals.reshape(blocks, STRETCH, head_count, head_width)
    step_heads = jnp.transpose(step_size.reshape(blocks, STRETCH, head_count), (0, 2, 1))
    log_cum = jnp.cumsum(jnp.transpose(log_rate.reshape(blocks, STRETCH, head_count), (0, 2, 1)), axis=2)
    write_blocks = write_proj.reshape(blocks, STRETCH, -1)
    read_blocks = read_proj.reshape(blocks, STRETCH, -1)
    seg_blocks = seg_row.reshape(blocks, STRETCH)
    positions = jnp.arange(STRETCH)
    causal = positions[:, None] >= positions[None, :]
    same_doc = (seg_blocks[:, :, None] == seg_blocks[:, None, :]) & causal[None]
    same_float = same_doc.astype(log_cum.dtype)[:, None]
    log_gap = log_cum[:, :, :, None] - log_cum[:, :, None, :]
    decay_mat = jnp.exp(jnp.where(same_doc[:, None], log_gap, 0.0)) * same_float
    scores = jnp.einsum('btn,bsn->bts', read_blocks, write_blocks, precision=highest)
    weighted = decay_mat * scores[:, None] * step_heads[:, :, None, :]
    within = jnp.einsum('bhts,bshp->bthp', weighted, block_vals, precision=highest)
    end_same = (seg_blocks == seg_blocks[:, -1:]).astype(log_cum.dtype)
    to_end = jnp.exp(log_cum[:, :, -1:] - log_cum) * end_same[:, None, :] * step_heads
    block_states = jnp.einsum('bhs,bshp,bsn->bhpn', to_end, block_vals, write_blocks, precision=highest)
    carried = block_states[0]
    outputs = [jnp.zeros_like(within[0])]
    for block_idx in range(1, blocks):
        link = (seg_blocks[block_idx] == seg_blocks[block_idx - 1, -1]).astype(log_cum.dtype)
        enter_gain = jnp.exp(log_cum[block_idx]) * link[None, :]
        carried_out = jnp.einsum('tn,hpn->thp', read_blocks[block_idx], carried, precision=highest)
        outputs.append(carried_out * jnp.transpose(enter_gain)[:, :, None])
        keep_gain = jnp.exp(log_cum[block_idx, :, -1]) * link[-1]
        carried = keep_gain[:, None, None] * carried + block_states[block_idx]
    return (within + jnp.stack(outputs)).reshape(length, head_count, head_width)

def mix_one(proj, conv_arr, head_arr, gate_arr, seg_row):
    length = proj.shape[0]
    inner_width = gate_arr.shape[0]
    head_count = head_arr.shape[1]
    conv_width = conv_arr.shape[1]
    kernel = conv_arr.shape[0] - 1
    state_width = (conv_width - inner_width) // 2
    gate_cols = proj[:, :inner_width]
    conv_input = proj[:, inner_width:inner_width + conv_width]
    step_raw = proj[:, inner_width + conv_width:]
    summed = conv_arr[kernel] + conv_arr[kernel - 1] * conv_input
    for offset in range(1, kernel):
        shifted = jnp.concatenate([jnp.zeros((offset, conv_width), proj.dtype), conv_input[:length - offset]], axis=0)
        seg_before = jnp.concatenate([jnp.full((offset,), -1, jnp.int32), seg_row[:length - offset].astype(jnp.int32)])
        keep_mask = (seg_before == seg_row.astype(jnp.int32)).astype(proj.dtype)[:, None]
        summed = summed + conv_arr[kernel - 1 - offset] * shifted * keep_mask
    activated = jax.nn.silu(summed)
    head_vals = activated[:, :inner_width].reshape(length, head_count, inner_width // head_count)
    write_proj = activated[:, inner_width:inner_width + state_width]
    read_proj = activated[:, inner_width + state_width:]
    step_size = jax.nn.softplus(step_raw + head_arr[0])
    log_rate = -step_size * jnp.exp(head_arr[1])
    scanned = scan_blocks(head_vals, step_size, log_rate, write_proj, read_proj, seg_row)
    scanned = scanned + head_arr[2][None, :, None] * head_vals
    gated = scanned.reshape(length, inner_width) * jax.nn.silu(gate_cols)
    return norm_rows(gated, gate_arr)

def adam_update(master, moments, grad_arr, clip_factor):
    clipped = grad_arr * clip_factor
    first = beta_first * moments[0] + (1.0 - beta_first) * clipped
    second_root = jnp.sqrt(beta_second * moments[1] * moments[1] + (1.0 - beta_second) * clipped * clipped)
    first_hat = first / (1.0 - beta_first ** STEP)
    root_hat = second_root / jnp.sqrt(1.0 - beta_second ** STEP)
    updated = master - learn_rate * (first_hat / (root_hat + adam_eps) + weight_decay * master)
    return (updated, jnp.stack([first, second_root]))

def reference(inputs, segment_ids, out_grad, norm_gain, in_weight, conv_params, head_params, gate_gain, out_weight, norm_gain_moments, in_weight_moments, conv_params_moments, head_params_moments, gate_gain_moments, out_weight_moments):
    wide = jnp.float32
    half = jnp.bfloat16
    norm_half = norm_gain.astype(half)
    in_half = in_weight.astype(half)
    conv_half = conv_params.astype(half)
    head_half = head_params.astype(half)
    gate_half = gate_gain.astype(half)
    out_half = out_weight.astype(half)
    norm_wide = norm_half.astype(wide)
    conv_wide = conv_half.astype(wide)
    head_wide = head_half.astype(wide)
    gate_wide = gate_half.astype(wide)

    def one_sequence(totals, item_set):
        seq_inputs, seq_ids, seq_grad = item_set
        input_wide = seq_inputs.astype(wide)
        normed = norm_rows(input_wide, norm_wide).astype(half)
        proj = jnp.dot(normed, in_half, preferred_element_type=wide)

        def mixer(proj_arg, conv_arg, head_arg, gate_arg):
            return mix_one(proj_arg, conv_arg, head_arg, gate_arg, seq_ids)
        mixed_out, mixer_back = jax.vjp(mixer, proj, conv_wide, head_wide, gate_wide)
        mixed_half = mixed_out.astype(half)
        block_seq = (input_wide + jnp.dot(mixed_half, out_half, preferred_element_type=wide)).astype(half)
        grad_out_w = jnp.dot(mixed_half.T, seq_grad, preferred_element_type=wide)
        d_mixed = jnp.dot(seq_grad, out_half.T, preferred_element_type=wide)
        d_proj, grad_conv, grad_head, grad_gate = mixer_back(d_mixed)
        dproj_half = d_proj.astype(half)
        grad_in_w = jnp.dot(normed.T, dproj_half, preferred_element_type=wide)
        d_normed = jnp.dot(dproj_half, in_half.T, preferred_element_type=wide)
        norm_back = jax.vjp(norm_rows, input_wide, norm_wide)[1]
        d_input, grad_norm = norm_back(d_normed)
        input_seq_grad = seq_grad.astype(wide) + d_input
        new_totals = (totals[0] + grad_norm, totals[1] + grad_in_w, totals[2] + grad_conv, totals[3] + grad_head, totals[4] + grad_gate, totals[5] + grad_out_w)
        return (new_totals, (block_seq, input_seq_grad))
    zeros = (jnp.zeros(norm_gain.shape, wide), jnp.zeros(in_weight.shape, wide), jnp.zeros(conv_params.shape, wide), jnp.zeros(head_params.shape, wide), jnp.zeros(gate_gain.shape, wide), jnp.zeros(out_weight.shape, wide))
    totals, stacked = lax.scan(one_sequence, zeros, (inputs, segment_ids, out_grad))
    block_all, input_all = stacked
    squares = jnp.sum(totals[0] * totals[0])
    for grad_arr in totals[1:]:
        squares = squares + jnp.sum(grad_arr * grad_arr)
    clip_factor = jnp.minimum(1.0, clip_limit / jnp.sqrt(squares + 1e-06))
    norm_new, norm_mom = adam_update(norm_gain, norm_gain_moments, totals[0], clip_factor)
    in_new, in_mom = adam_update(in_weight, in_weight_moments, totals[1], clip_factor)
    conv_new, conv_mom = adam_update(conv_params, conv_params_moments, totals[2], clip_factor)
    head_new, head_mom = adam_update(head_params, head_params_moments, totals[3], clip_factor)
    gate_new, gate_mom = adam_update(gate_gain, gate_gain_moments, totals[4], clip_factor)
    out_new, out_mom = adam_update(out_weight, out_weight_moments, totals[5], clip_factor)
    return (block_all, input_all, totals[0], totals[1], totals[2], totals[3], totals[4], totals[5], norm_new, in_new, conv_new, head_new, gate_new, out_new, norm_mom, in_mom, conv_mom, head_mom, gate_mom, out_mom)
```

```python
import jax
import jax.numpy as jnp
from jax import lax
from jax.experimental import pallas as pl
from jax.experimental.pallas import tpu as pltpu
from jax.sharding import PartitionSpec as P

STRETCH = 256
STEP = 5


norm_eps = 1e-05
clip_limit = 1.0
beta_first = 0.9
beta_second = 0.999
adam_eps = 1e-08
learn_rate = 0.02
weight_decay = 0.1


def norm_rows(features, gain_vec):
    inverse = lax.rsqrt(jnp.mean(features * features, axis=-1, keepdims=True) + norm_eps)
    return features * inverse * gain_vec


def scan_blocks(head_vals, step_size, log_rate, write_proj, read_proj, seg_row):
    highest = lax.Precision.HIGHEST
    length, head_count, head_width = head_vals.shape
    blocks = length // STRETCH
    block_vals = head_vals.reshape(blocks, STRETCH, head_count, head_width)
    step_heads = jnp.transpose(step_size.reshape(blocks, STRETCH, head_count), (0, 2, 1))
    log_cum = jnp.cumsum(
        jnp.transpose(log_rate.reshape(blocks, STRETCH, head_count), (0, 2, 1)), axis=2
    )
    write_blocks = write_proj.reshape(blocks, STRETCH, -1)
    read_blocks = read_proj.reshape(blocks, STRETCH, -1)
    seg_blocks = seg_row.reshape(blocks, STRETCH)
    positions = jnp.arange(STRETCH)
    causal = positions[:, None] >= positions[None, :]
    same_doc = (seg_blocks[:, :, None] == seg_blocks[:, None, :]) & causal[None]
    log_gap = jnp.where(
        same_doc[:, None], log_cum[:, :, :, None] - log_cum[:, :, None, :], -jnp.inf
    )
    scores = jnp.einsum("btn,bsn->bts", read_blocks, write_blocks, precision=highest)
    weighted = jnp.exp(log_gap) * scores[:, None] * step_heads[:, :, None, :]
    within = jnp.einsum("bhts,bshp->bthp", weighted, block_vals, precision=highest)
    end_same = (seg_blocks == seg_blocks[:, -1:]).astype(log_cum.dtype)
    to_end = jnp.exp(log_cum[:, :, -1:] - log_cum) * end_same[:, None, :] * step_heads
    block_states = jnp.einsum(
        "bhs,bshp,bsn->bhpn", to_end, block_vals, write_blocks, precision=highest
    )
    carried = block_states[0]
    outputs = [jnp.zeros_like(within[0])]
    return (within + jnp.stack(outputs)).reshape(length, head_count, head_width)


def mix_one(proj, conv_arr, head_arr, gate_arr, seg_row):
    length = proj.shape[0]
    inner_width = gate_arr.shape[0]
    head_count = head_arr.shape[1]
    conv_width = conv_arr.shape[1]
    kernel = conv_arr.shape[0] - 1
    state_width = (conv_width - inner_width) // 2
    gate_cols = proj[:, :inner_width]
    conv_input = proj[:, inner_width : inner_width + conv_width]
    step_raw = proj[:, inner_width + conv_width :]
    summed = conv_arr[kernel] + conv_arr[kernel - 1] * conv_input
    for offset in range(1, kernel):
        shifted = jnp.concatenate(
            [jnp.zeros((offset, conv_width), proj.dtype), conv_input[: length - offset]], axis=0
        )
        seg_before = jnp.concatenate(
            [jnp.full((offset,), -1, jnp.int32), seg_row[: length - offset]]
        )
        keep_mask = (seg_before == seg_row).astype(proj.dtype)[:, None]
        summed = summed + conv_arr[kernel - 1 - offset] * shifted * keep_mask
    activated = jax.nn.silu(summed)
    head_vals = activated[:, :inner_width].reshape(length, head_count, inner_width // head_count)
    write_proj = activated[:, inner_width : inner_width + state_width]
    read_proj = activated[:, inner_width + state_width :]
    step_size = jax.nn.softplus(step_raw + head_arr[0])
    log_rate = -step_size * jnp.exp(head_arr[1])
    scanned = scan_blocks(head_vals, step_size, log_rate, write_proj, read_proj, seg_row)
    scanned = scanned + head_arr[2][None, :, None] * head_vals
    gated = scanned.reshape(length, inner_width) * jax.nn.silu(gate_cols)
    return norm_rows(gated, gate_arr)


def adam_update(master, moments, grad_arr, clip_factor):
    clipped = grad_arr * clip_factor
    first = beta_first * moments[0] + (1.0 - beta_first) * clipped
    second_root = jnp.sqrt(
        beta_second * moments[1] * moments[1] + (1.0 - beta_second) * clipped * clipped
    )
    first_hat = first / (1.0 - beta_first**STEP)
    root_hat = second_root / jnp.sqrt(1.0 - beta_second**STEP)
    updated = master - learn_rate * (first_hat / (root_hat + adam_eps) + weight_decay * master)
    return (updated, jnp.stack([first, second_root]))


def square_sum(arrays):
    total = jnp.zeros((), jnp.float32)
    for grad_arr in arrays:
        total = total + jnp.sum(grad_arr * grad_arr)
    return total


MESH = pl.DeviceIdType.MESH
BITS = 3
SLAB = 16


def chunks_of(shapes):
    found = []
    for which, (_, cols) in enumerate(shapes):
        width = 768 if which == 0 else 384
        start = 0
        while start < cols:
            found.append((which, start, min(width, cols - start)))
            start += width
    order = sorted(found, key=lambda item: -item[2] * shapes[item[0]][0])
    return tuple(order)


def reduce_body(shapes, plan, *refs):
    count = len(shapes)
    grads = refs[:count]
    finals = refs[count : 2 * count]
    scratch = refs[2 * count : 2 * count + 6 * count]
    pair_in, half_out, half_in, first_in, second_in, third_in = [
        scratch[k * count : (k + 1) * count] for k in range(6)
    ]
    send_sem, recv_sem = refs[-2:]
    grp, dp = lax.axis_index("grp"), lax.axis_index("dp")
    core, cross = lax.rem(grp, 2), lax.div(grp, 2)
    other_core, other_cross = 1 - core, 1 - cross
    bit_vals = [lax.rem(lax.div(dp, 1 << k), 2) for k in range(BITS)]
    core_dev = {"grp": cross * 2 + other_core, "dp": dp}
    cross_dev = {"grp": other_cross * 2 + core, "dp": dp}
    dp_devs = [
        {"grp": grp, "dp": dp + (1 - 2 * bit_vals[k]) * (1 << k)} for k in range(BITS)
    ]
    barrier = pltpu.get_barrier_semaphore()
    for device in [core_dev, cross_dev] + dp_devs:
        pl.semaphore_signal(barrier, inc=1, device_id=device, device_id_type=MESH)
    pl.semaphore_wait(barrier, 2 + BITS)

    def span(start, rows):
        return pl.ds(pl.multiple_of(start, 8), rows)

    def remote(src, dst, chunk, slot, device):
        copy = pltpu.make_async_remote_copy(
            src_ref=src,
            dst_ref=dst,
            send_sem=send_sem.at[chunk, slot],
            recv_sem=recv_sem.at[chunk, slot],
            device_id=device,
            device_id_type=MESH,
        )
        copy.start()
        return copy

    copies = {}
    for chunk, (which, start, width) in enumerate(plan):
        rows = shapes[which][0] // 4
        cols = slice(start, start + width)
        for keep in range(2):
            origin = (2 * keep + other_core) * rows
            copies[chunk, keep] = remote(
                grads[which].at[span(origin, rows), cols],
                pair_in[which].at[keep, :, cols],
                chunk,
                keep,
                core_dev,
            )

    def tiles(rows, step):
        height = SLAB if rows % SLAB == 0 else 8

        @pl.loop(0, rows // height)
        def _(index):
            step(index * height, height)

    def offset_to(which, levels):
        rows = shapes[which][0] // 4
        total = 0
        for k in range(levels):
            total = total + bit_vals[k] * (rows >> (k + 1))
        return total

    def stage(chunk, number):
        which, start, width = plan[chunk]
        rows = shapes[which][0] // 4
        cols = slice(start, start + width)
        grad, final = grads[which], finals[which]
        pair, out_half, in_half = pair_in[which], half_out[which], half_in[which]
        level_in = [first_in[which], second_in[which], third_in[which]]
        if number == 0:
            copies[chunk, 0].wait_recv()
            copies[chunk, 1].wait_recv()

            def send_part(base, height):
                own = grad[span((2 * other_cross + core) * rows + base, height), cols]
                got = pair[other_cross, span(base, height), cols]
                out_half[span(base, height), cols] = (own + got).astype(out_half.dtype)

            tiles(rows, send_part)
            copies[chunk, 2] = remote(
                out_half.at[:, cols], in_half.at[:, cols], chunk, 2, cross_dev
            )

            def keep_part(base, height):
                own = grad[span((2 * cross + core) * rows + base, height), cols]
                pair[cross, span(base, height), cols] += own

            tiles(rows, keep_part)
        elif number == 1:
            copies[chunk, 2].wait_recv()
            half = rows // 2

            def add_cross(base, height):
                got = in_half[span(base, height), cols].astype(jnp.float32)
                pair[cross, span(base, height), cols] += got

            tiles(rows, add_cross)
            copies[chunk, 3] = remote(
                pair.at[cross, span((1 - bit_vals[0]) * half, half), cols],
                level_in[0].at[:, cols],
                chunk,
                3,
                dp_devs[0],
            )
        elif number < 1 + BITS:
            level = number - 2
            size = rows >> (level + 1)
            copies[chunk, 3 + level].wait_recv()
            target = level_in[level]

            def add_level(base, height):
                if level == 0:
                    own = pair[cross, span(bit_vals[0] * size + base, height), cols]
                else:
                    own = level_in[level - 1][span(bit_vals[level] * size + base, height), cols]
                target[span(base, height), cols] += own

            tiles(size, add_level)
            half = size // 2
            copies[chunk, 4 + level] = remote(
                target.at[span((1 - bit_vals[level + 1]) * half, half), cols],
                level_in[level + 1].at[:, cols],
                chunk,
                4 + level,
                dp_devs[level + 1],
            )
        elif number == 1 + BITS:
            level = BITS - 1
            size = rows >> BITS
            copies[chunk, 3 + level].wait_recv()
            place = offset_to(which, BITS)

            def add_last(base, height):
                own = level_in[level - 1][span(bit_vals[level] * size + base, height), cols]
                got = level_in[level][span(base, height), cols]
                final[span(place + base, height), cols] = own + got

            tiles(size, add_last)
            gather(chunk, 0)
        else:
            done = number - 2 - BITS
            copies[chunk, 3 + BITS + done].wait_recv()
            if done < BITS - 1:
                gather(chunk, done + 1)

    def gather(chunk, number):
        which, start, width = plan[chunk]
        rows = shapes[which][0] // 4
        levels = BITS - number
        size = rows >> levels
        piece = finals[which].at[span(offset_to(which, levels), size), start : start + width]
        copies[chunk, 3 + BITS + number] = remote(
            piece, piece, chunk, 3 + BITS + number, dp_devs[levels - 1]
        )

    stages = 2 + 2 * BITS
    for tick in range(len(plan) + stages - 1):
        for number in reversed(range(stages)):
            chunk = tick - number
            if 0 <= chunk < len(plan):
                stage(chunk, number)
    for copy in copies.values():
        copy.wait_send()


def reduce_grads(arrays):
    shapes = tuple(array.shape for array in arrays)
    plan = chunks_of(shapes)
    wide = jnp.float32
    kinds = (jnp.bfloat16, jnp.bfloat16, jnp.float32)
    quarter = [(rows // 4, cols) for rows, cols in shapes]
    scratch = [pltpu.VMEM((2,) + size, wide) for size in quarter]
    scratch += [pltpu.VMEM(size, kind) for size, kind in zip(quarter, kinds)]
    scratch += [pltpu.VMEM(size, kind) for size, kind in zip(quarter, kinds)]
    for level in range(BITS):
        scratch += [pltpu.VMEM((rows >> (level + 1), cols), wide) for rows, cols in quarter]
    slots = 3 + 2 * BITS
    scratch += [pltpu.SemaphoreType.DMA((len(plan), slots))] * 2
    return pl.pallas_call(
        lambda *refs: reduce_body(shapes, plan, *refs),
        out_shape=[jax.ShapeDtypeStruct(size, wide) for size in quarter],
        in_specs=[pl.BlockSpec(memory_space=pltpu.VMEM)] * len(shapes),
        out_specs=[pl.BlockSpec(memory_space=pltpu.VMEM)] * len(shapes),
        scratch_shapes=scratch,
        compiler_params=pltpu.CompilerParams(
            collective_id=0, has_side_effects=True, vmem_limit_bytes=58 * 1024 * 1024
        ),
        name="reduce_grads",
    )(*arrays)


def shards(
    inputs,
    segment_ids,
    out_grad,
    norm_gain,
    in_weight,
    conv_params,
    head_params,
    gate_gain,
    out_weight,
    norm_gain_moments,
    in_weight_moments,
    conv_params_moments,
    head_params_moments,
    gate_gain_moments,
    out_weight_moments,
):
    wide = jnp.float32
    half = jnp.bfloat16
    norm_half, in_half, conv_half, head_half, gate_half, out_half = (
        lax.all_gather(norm_gain.astype(half), "grp", axis=0, tiled=True),
        lax.all_gather(in_weight.astype(half), "grp", axis=0, tiled=True),
        lax.all_gather(conv_params.astype(half), "grp", axis=1, tiled=True),
        lax.all_gather(head_params.astype(half), "grp", axis=1, tiled=True),
        lax.all_gather(gate_gain.astype(half), "grp", axis=0, tiled=True),
        lax.all_gather(out_weight.astype(half), "grp", axis=0, tiled=True),
    )
    seq_count, length, width = inputs.shape
    row_count = seq_count * length
    input_wide = inputs.reshape(row_count, width).astype(wide)
    norm_wide = norm_half.astype(wide)
    conv_wide = conv_half.astype(wide)
    head_wide = head_half.astype(wide)
    gate_wide = gate_half.astype(wide)
    normed = norm_rows(input_wide, norm_wide).astype(half)
    proj = jnp.dot(normed, in_half, preferred_element_type=wide).reshape(seq_count, length, -1)

    def mixer(proj_arg, conv_arg, head_arg, gate_arg):
        return jax.vmap(
            lambda proj_row, seg_row: mix_one(proj_row, conv_arg, head_arg, gate_arg, seg_row)
        )(proj_arg, segment_ids)

    mixed_out, mixer_back = jax.vjp(mixer, proj, conv_wide, head_wide, gate_wide)
    mixed_half = mixed_out.reshape(row_count, -1).astype(half)
    block_rows = input_wide + jnp.dot(mixed_half, out_half, preferred_element_type=wide)
    block_out = block_rows.astype(half).reshape(seq_count, length, width)
    cotangent = out_grad.reshape(row_count, width)
    out_w_local = jnp.einsum("ti,td->id", mixed_half, cotangent, preferred_element_type=wide)
    d_mixed = jnp.einsum("td,id->ti", cotangent, out_half, preferred_element_type=wide)
    d_proj, grad_conv, grad_head, grad_gate = mixer_back(d_mixed.reshape(seq_count, length, -1))
    dproj_half = d_proj.reshape(row_count, -1).astype(half)
    main_cols = dproj_half.shape[1] // 128 * 128
    grad_main = jnp.einsum(
        "td,tk->dk", normed, dproj_half[:, :main_cols], preferred_element_type=wide
    )
    grad_tail = jnp.einsum(
        "td,tk->dk", normed, dproj_half[:, main_cols:], preferred_element_type=wide
    )
    d_normed = jnp.einsum("tk,dk->td", dproj_half, in_half, preferred_element_type=wide)
    norm_back = jax.vjp(norm_rows, input_wide, norm_wide)[1]
    d_input, grad_norm = norm_back(d_normed)
    input_grad = (cotangent.astype(wide) + d_input).reshape(seq_count, length, width)
    grp_size = 4
    own_rows = width // grp_size
    conv_cols = grad_conv.shape[1] // grp_size
    head_cols = grad_head.shape[1] // grp_size
    gate_size = grad_gate.shape[0] // grp_size
    small = [
        grad_norm.reshape(grp_size, -1),
        grad_gate.reshape(grp_size, -1),
        jnp.transpose(grad_conv.reshape(-1, grp_size, conv_cols), (1, 0, 2)).reshape(grp_size, -1),
        jnp.transpose(grad_head.reshape(-1, grp_size, head_cols), (1, 0, 2)).reshape(grp_size, -1),
    ]
    small = jnp.concatenate(small, axis=1)
    small_size = small.shape[1]
    tail_cols = grad_tail.shape[1]
    spare = 128 - tail_cols
    small = jnp.pad(small, ((0, 0), (0, own_rows * spare - small_size)))
    small = small.reshape(grp_size * own_rows, spare)
    grad_last = jnp.concatenate([grad_tail, small], axis=1)
    reduced = reduce_grads((grad_main, out_w_local, grad_last))
    groups = lax.axis_size("dp")
    step = 1 << BITS
    while step < groups:
        pairs = [(index, index ^ step) for index in range(groups)]
        reduced = [piece + lax.ppermute(piece, "dp", pairs) for piece in reduced]
        step *= 2
    main_sum, out_grad_w, last_sum = reduced
    in_grad = jnp.concatenate([main_sum, last_sum[:, :tail_cols]], axis=1)
    flat = last_sum[:, tail_cols:].reshape(-1)
    norm_grad = flat[:own_rows]
    gate_grad = flat[own_rows : own_rows + gate_size]
    conv_at = own_rows + gate_size
    head_at = conv_at + grad_conv.shape[0] * conv_cols
    conv_grad = flat[conv_at:head_at].reshape(-1, conv_cols)
    head_grad = flat[head_at:small_size].reshape(-1, head_cols)
    local_squares = square_sum((norm_grad, in_grad, conv_grad, head_grad, gate_grad, out_grad_w))
    squares = lax.psum(local_squares, "grp")
    clip_factor = jnp.minimum(1.0, clip_limit / jnp.sqrt(squares + 1e-06))
    norm_new, norm_mom = adam_update(norm_gain, norm_gain_moments, norm_grad, clip_factor)
    in_new, in_mom = adam_update(in_weight, in_weight_moments, in_grad, clip_factor)
    conv_new, conv_mom = adam_update(conv_params, conv_params_moments, conv_grad, clip_factor)
    head_new, head_mom = adam_update(head_params, head_params_moments, head_grad, clip_factor)
    gate_new, gate_mom = adam_update(gate_gain, gate_gain_moments, gate_grad, clip_factor)
    out_new, out_mom = adam_update(out_weight, out_weight_moments, out_grad_w, clip_factor)
    return (
        block_out,
        input_grad,
        norm_grad,
        in_grad,
        conv_grad,
        head_grad,
        gate_grad,
        out_grad_w,
        norm_new,
        in_new,
        conv_new,
        head_new,
        gate_new,
        out_new,
        norm_mom,
        in_mom,
        conv_mom,
        head_mom,
        gate_mom,
        out_mom,
    )


def solution(mesh):
    in_specs = (
        P(("grp", "dp"), None, None),
        P(("grp", "dp"), None),
        P(("grp", "dp"), None, None),
        P("grp"),
        P("grp", None),
        P(None, "grp"),
        P(None, "grp"),
        P("grp"),
        P("grp", None),
        P(None, "grp"),
        P(None, "grp", None),
        P(None, None, "grp"),
        P(None, None, "grp"),
        P(None, "grp"),
        P(None, "grp", None),
    )
    out_specs = (
        P(("grp", "dp"), None, None),
        P(("grp", "dp"), None, None),
        P("grp"),
        P("grp", None),
        P(None, "grp"),
        P(None, "grp"),
        P("grp"),
        P("grp", None),
        P("grp"),
        P("grp", None),
        P(None, "grp"),
        P(None, "grp"),
        P("grp"),
        P("grp", None),
        P(None, "grp"),
        P(None, "grp", None),
        P(None, None, "grp"),
        P(None, None, "grp"),
        P(None, "grp"),
        P(None, "grp", None),
    )
    return jax.shard_map(shards, mesh=mesh, in_specs=in_specs, out_specs=out_specs, check_vma=False)
```

```python
import jax
import jax.numpy as jnp
from jax import lax
from jax.experimental import pallas as pl
from jax.experimental.pallas import tpu as pltpu
from jax.sharding import PartitionSpec as P

STRETCH = 256
STEP = 5


norm_eps = 1e-05
clip_limit = 1.0
beta_first = 0.9
beta_second = 0.999
adam_eps = 1e-08
learn_rate = 0.02
weight_decay = 0.1


def norm_rows(features, gain_vec):
    inverse = lax.rsqrt(jnp.mean(features * features, axis=-1, keepdims=True) + norm_eps)
    return features * inverse * gain_vec


def scan_blocks(head_vals, step_size, log_rate, write_proj, read_proj, seg_row):
    highest = lax.Precision.HIGH
    length, head_count, head_width = head_vals.shape
    blocks = length // STRETCH
    block_vals = head_vals.reshape(blocks, STRETCH, head_count, head_width)
    step_heads = jnp.transpose(step_size.reshape(blocks, STRETCH, head_count), (0, 2, 1))
    log_cum = jnp.cumsum(
        jnp.transpose(log_rate.reshape(blocks, STRETCH, head_count), (0, 2, 1)), axis=2
    )
    write_blocks = write_proj.reshape(blocks, STRETCH, -1)
    read_blocks = read_proj.reshape(blocks, STRETCH, -1)
    seg_blocks = seg_row.reshape(blocks, STRETCH)
    positions = jnp.arange(STRETCH)
    causal = positions[:, None] >= positions[None, :]
    same_doc = (seg_blocks[:, :, None] == seg_blocks[:, None, :]) & causal[None]
    log_gap = jnp.where(
        same_doc[:, None], log_cum[:, :, :, None] - log_cum[:, :, None, :], -jnp.inf
    )
    scores = jnp.einsum("btn,bsn->bts", read_blocks, write_blocks, precision=highest)
    weighted = jnp.exp(log_gap) * scores[:, None] * step_heads[:, :, None, :]
    within = jnp.einsum("bhts,bshp->bthp", weighted, block_vals, precision=highest)
    end_same = (seg_blocks == seg_blocks[:, -1:]).astype(log_cum.dtype)
    to_end = jnp.exp(log_cum[:, :, -1:] - log_cum) * end_same[:, None, :] * step_heads
    block_states = jnp.einsum(
        "bhs,bshp,bsn->bhpn", to_end, block_vals, write_blocks, precision=highest
    )
    carried = block_states[0]
    outputs = [jnp.zeros_like(within[0])]
    return (within + jnp.stack(outputs)).reshape(length, head_count, head_width)


def mix_one(proj, conv_arr, head_arr, gate_arr, seg_row):
    length = proj.shape[0]
    inner_width = gate_arr.shape[0]
    head_count = head_arr.shape[1]
    conv_width = conv_arr.shape[1]
    kernel = conv_arr.shape[0] - 1
    state_width = (conv_width - inner_width) // 2
    gate_cols = proj[:, :inner_width]
    conv_input = proj[:, inner_width : inner_width + conv_width]
    step_raw = proj[:, inner_width + conv_width :]
    summed = conv_arr[kernel] + conv_arr[kernel - 1] * conv_input
    for offset in range(1, kernel):
        shifted = jnp.concatenate(
            [jnp.zeros((offset, conv_width), proj.dtype), conv_input[: length - offset]], axis=0
        )
        seg_before = jnp.concatenate(
            [jnp.full((offset,), -1, jnp.int32), seg_row[: length - offset]]
        )
        keep_mask = (seg_before == seg_row).astype(proj.dtype)[:, None]
        summed = summed + conv_arr[kernel - 1 - offset] * shifted * keep_mask
    activated = jax.nn.silu(summed)
    head_vals = activated[:, :inner_width].reshape(length, head_count, inner_width // head_count)
    write_proj = activated[:, inner_width : inner_width + state_width]
    read_proj = activated[:, inner_width + state_width :]
    step_size = jax.nn.softplus(step_raw + head_arr[0])
    log_rate = -step_size * jnp.exp(head_arr[1])
    scanned = scan_blocks(head_vals, step_size, log_rate, write_proj, read_proj, seg_row)
    scanned = scanned + head_arr[2][None, :, None] * head_vals
    gated = scanned.reshape(length, inner_width) * jax.nn.silu(gate_cols)
    return norm_rows(gated, gate_arr)


def adam_update(master, moments, grad_arr, clip_factor):
    clipped = grad_arr * clip_factor
    first = beta_first * moments[0] + (1.0 - beta_first) * clipped
    second_root = jnp.sqrt(
        beta_second * moments[1] * moments[1] + (1.0 - beta_second) * clipped * clipped
    )
    first_hat = first / (1.0 - beta_first**STEP)
    root_hat = second_root / jnp.sqrt(1.0 - beta_second**STEP)
    updated = master - learn_rate * (first_hat / (root_hat + adam_eps) + weight_decay * master)
    return (updated, jnp.stack([first, second_root]))


def update_body(count, widths, clip_ref, *refs):
    grads = refs[:count]
    master_ref, moment_ref, grad_out, master_out, moment_out = refs[count:]
    clip_factor = clip_ref[0, 0]
    start = 0
    for grad_ref, width in zip(grads, widths):
        cols = slice(start, start + width)
        grad = grad_ref[:, :width]
        master = master_ref[:, cols]
        grad_out[:, cols] = grad
        clipped = grad * clip_factor
        first = beta_first * moment_ref[0, :, cols] + (1.0 - beta_first) * clipped
        root = moment_ref[1, :, cols]
        second_root = jnp.sqrt(beta_second * root * root + (1.0 - beta_second) * clipped * clipped)
        first_hat = first / (1.0 - beta_first**STEP)
        root_hat = second_root / ((1.0 - beta_second**STEP) ** 0.5)
        step = first_hat / (root_hat + adam_eps) + weight_decay * master
        master_out[:, cols] = master - learn_rate * step
        moment_out[0, :, cols] = first
        moment_out[1, :, cols] = second_root
        start += width


def update_weight(master, moments, grads, widths, clip_factor, name):
    rows, cols = master.shape
    height = 24 if rows % 24 == 0 else rows
    if cols < 1024 and rows % 96 == 0:
        height = 96
    wide = jnp.float32
    row_spec = pl.BlockSpec((height, cols), lambda i: (i, 0))
    pair_spec = pl.BlockSpec((2, height, cols), lambda i: (0, i, 0))
    return pl.pallas_call(
        lambda *refs: update_body(len(grads), widths, *refs),
        grid=(rows // height,),
        out_shape=[
            jax.ShapeDtypeStruct((rows, cols), wide),
            jax.ShapeDtypeStruct((rows, cols), wide),
            jax.ShapeDtypeStruct((2, rows, cols), wide),
        ],
        in_specs=[pl.BlockSpec(memory_space=pltpu.SMEM)]
        + [pl.BlockSpec((height, grad.shape[1]), lambda i: (i, 0)) for grad in grads]
        + [row_spec, pair_spec],
        out_specs=[row_spec, row_spec, pair_spec],
        compiler_params=pltpu.CompilerParams(vmem_limit_bytes=40 * 1024 * 1024),
        name=name,
    )(clip_factor.reshape(1, 1), *grads, master, moments)


def square_sum(arrays):
    total = jnp.zeros((), jnp.float32)
    for grad_arr in arrays:
        total = total + jnp.sum(grad_arr * grad_arr)
    return total


MESH = pl.DeviceIdType.MESH
BITS = 3
SLAB = 16


def chunks_of(shapes):
    found = []
    for which, (_, cols) in enumerate(shapes):
        width = 768 if which == 0 else 384
        start = 0
        while start < cols:
            found.append((which, start, min(width, cols - start)))
            start += width
    order = sorted(found, key=lambda item: -item[2] * shapes[item[0]][0])
    return tuple(order)


def reduce_body(shapes, plan, *refs):
    count = len(shapes)
    grads = refs[:count]
    finals = refs[count : 2 * count]
    scratch = refs[2 * count : 2 * count + 6 * count]
    pair_in, half_out, half_in, first_in, second_in, third_in = [
        scratch[k * count : (k + 1) * count] for k in range(6)
    ]
    send_sem, recv_sem = refs[-2:]
    grp, dp = lax.axis_index("grp"), lax.axis_index("dp")
    core, cross = lax.rem(grp, 2), lax.div(grp, 2)
    other_core, other_cross = 1 - core, 1 - cross
    bit_vals = [lax.rem(lax.div(dp, 1 << k), 2) for k in range(BITS)]
    core_dev = {"grp": cross * 2 + other_core, "dp": dp}
    cross_dev = {"grp": other_cross * 2 + core, "dp": dp}
    dp_devs = [
        {"grp": grp, "dp": dp + (1 - 2 * bit_vals[k]) * (1 << k)} for k in range(BITS)
    ]
    barrier = pltpu.get_barrier_semaphore()
    for device in [core_dev, cross_dev] + dp_devs:
        pl.semaphore_signal(barrier, inc=1, device_id=device, device_id_type=MESH)
    pl.semaphore_wait(barrier, 2 + BITS)

    def span(start, rows):
        return pl.ds(pl.multiple_of(start, 8), rows)

    def remote(src, dst, chunk, slot, device):
        copy = pltpu.make_async_remote_copy(
            src_ref=src,
            dst_ref=dst,
            send_sem=send_sem.at[chunk, slot],
            recv_sem=recv_sem.at[chunk, slot],
            device_id=device,
            device_id_type=MESH,
        )
        copy.start()
        return copy

    copies = {}
    for chunk, (which, start, width) in enumerate(plan):
        rows = shapes[which][0] // 4
        cols = slice(start, start + width)
        for keep in range(2):
            origin = (2 * keep + other_core) * rows
            copies[chunk, keep] = remote(
                grads[which].at[span(origin, rows), cols],
                pair_in[which].at[keep, :, cols],
                chunk,
                keep,
                core_dev,
            )

    def tiles(rows, step):
        height = SLAB if rows % SLAB == 0 else 8

        @pl.loop(0, rows // height)
        def _(index):
            step(index * height, height)

    def offset_to(which, levels):
        rows = shapes[which][0] // 4
        total = 0
        for k in range(levels):
            total = total + bit_vals[k] * (rows >> (k + 1))
        return total

    def stage(chunk, number):
        which, start, width = plan[chunk]
        rows = shapes[which][0] // 4
        cols = slice(start, start + width)
        grad, final = grads[which], finals[which]
        pair, out_half, in_half = pair_in[which], half_out[which], half_in[which]
        level_in = [first_in[which], second_in[which], third_in[which]]
        if number == 0:
            copies[chunk, 0].wait_recv()
            copies[chunk, 1].wait_recv()

            def send_part(base, height):
                own = grad[span((2 * other_cross + core) * rows + base, height), cols]
                got = pair[other_cross, span(base, height), cols]
                out_half[span(base, height), cols] = (own + got).astype(out_half.dtype)

            tiles(rows, send_part)
            copies[chunk, 2] = remote(
                out_half.at[:, cols], in_half.at[:, cols], chunk, 2, cross_dev
            )

            def keep_part(base, height):
                own = grad[span((2 * cross + core) * rows + base, height), cols]
                pair[cross, span(base, height), cols] += own

            tiles(rows, keep_part)
        elif number == 1:
            copies[chunk, 2].wait_recv()
            half = rows // 2

            def add_cross(base, height):
                got = in_half[span(base, height), cols].astype(jnp.float32)
                pair[cross, span(base, height), cols] += got

            tiles(rows, add_cross)
            copies[chunk, 3] = remote(
                pair.at[cross, span((1 - bit_vals[0]) * half, half), cols],
                level_in[0].at[:, cols],
                chunk,
                3,
                dp_devs[0],
            )
        elif number < 1 + BITS:
            level = number - 2
            size = rows >> (level + 1)
            copies[chunk, 3 + level].wait_recv()
            target = level_in[level]

            def add_level(base, height):
                if level == 0:
                    own = pair[cross, span(bit_vals[0] * size + base, height), cols]
                else:
                    own = level_in[level - 1][span(bit_vals[level] * size + base, height), cols]
                target[span(base, height), cols] += own

            tiles(size, add_level)
            half = size // 2
            copies[chunk, 4 + level] = remote(
                target.at[span((1 - bit_vals[level + 1]) * half, half), cols],
                level_in[level + 1].at[:, cols],
                chunk,
                4 + level,
                dp_devs[level + 1],
            )
        elif number == 1 + BITS:
            level = BITS - 1
            size = rows >> BITS
            copies[chunk, 3 + level].wait_recv()
            place = offset_to(which, BITS)

            def add_last(base, height):
                own = level_in[level - 1][span(bit_vals[level] * size + base, height), cols]
                got = level_in[level][span(base, height), cols]
                final[span(place + base, height), cols] = own + got

            tiles(size, add_last)
            gather(chunk, 0)
        else:
            done = number - 2 - BITS
            copies[chunk, 3 + BITS + done].wait_recv()
            if done < BITS - 1:
                gather(chunk, done + 1)

    def gather(chunk, number):
        which, start, width = plan[chunk]
        rows = shapes[which][0] // 4
        levels = BITS - number
        size = rows >> levels
        piece = finals[which].at[span(offset_to(which, levels), size), start : start + width]
        copies[chunk, 3 + BITS + number] = remote(
            piece, piece, chunk, 3 + BITS + number, dp_devs[levels - 1]
        )

    stages = 2 + 2 * BITS
    for tick in range(len(plan) + stages - 1):
        for number in reversed(range(stages)):
            chunk = tick - number
            if 0 <= chunk < len(plan):
                stage(chunk, number)
    for copy in copies.values():
        copy.wait_send()


def reduce_grads(arrays):
    shapes = tuple(array.shape for array in arrays)
    plan = chunks_of(shapes)
    wide = jnp.float32
    kinds = (jnp.bfloat16, jnp.bfloat16, jnp.float32)
    quarter = [(rows // 4, cols) for rows, cols in shapes]
    scratch = [pltpu.VMEM((2,) + size, wide) for size in quarter]
    scratch += [pltpu.VMEM(size, kind) for size, kind in zip(quarter, kinds)]
    scratch += [pltpu.VMEM(size, kind) for size, kind in zip(quarter, kinds)]
    for level in range(BITS):
        scratch += [pltpu.VMEM((rows >> (level + 1), cols), wide) for rows, cols in quarter]
    slots = 3 + 2 * BITS
    scratch += [pltpu.SemaphoreType.DMA((len(plan), slots))] * 2
    return pl.pallas_call(
        lambda *refs: reduce_body(shapes, plan, *refs),
        out_shape=[jax.ShapeDtypeStruct(size, wide) for size in quarter],
        in_specs=[pl.BlockSpec(memory_space=pltpu.VMEM)] * len(shapes),
        out_specs=[pl.BlockSpec(memory_space=pltpu.VMEM)] * len(shapes),
        scratch_shapes=scratch,
        compiler_params=pltpu.CompilerParams(
            collective_id=0, has_side_effects=True, vmem_limit_bytes=58 * 1024 * 1024
        ),
        name="reduce_grads",
    )(*arrays)


def shards(
    inputs,
    segment_ids,
    out_grad,
    norm_gain,
    in_weight,
    conv_params,
    head_params,
    gate_gain,
    out_weight,
    norm_gain_moments,
    in_weight_moments,
    conv_params_moments,
    head_params_moments,
    gate_gain_moments,
    out_weight_moments,
):
    wide = jnp.float32
    half = jnp.bfloat16
    norm_half, in_half, conv_half, head_half, gate_half, out_half = (
        lax.all_gather(norm_gain.astype(half), "grp", axis=0, tiled=True),
        lax.all_gather(in_weight.astype(half), "grp", axis=0, tiled=True),
        lax.all_gather(conv_params.astype(half), "grp", axis=1, tiled=True),
        lax.all_gather(head_params.astype(half), "grp", axis=1, tiled=True),
        lax.all_gather(gate_gain.astype(half), "grp", axis=0, tiled=True),
        lax.all_gather(out_weight.astype(half), "grp", axis=0, tiled=True),
    )
    seq_count, length, width = inputs.shape
    row_count = seq_count * length
    input_wide = inputs.reshape(row_count, width).astype(wide)
    norm_wide = norm_half.astype(wide)
    conv_wide = conv_half.astype(wide)
    head_wide = head_half.astype(wide)
    gate_wide = gate_half.astype(wide)
    normed = norm_rows(input_wide, norm_wide).astype(half)
    proj = jnp.dot(normed, in_half, preferred_element_type=wide).reshape(seq_count, length, -1)

    def mixer(proj_arg, conv_arg, head_arg, gate_arg):
        return jax.vmap(
            lambda proj_row, seg_row: mix_one(proj_row, conv_arg, head_arg, gate_arg, seg_row)
        )(proj_arg, segment_ids)

    mixed_out, mixer_back = jax.vjp(mixer, proj, conv_wide, head_wide, gate_wide)
    mixed_half = mixed_out.reshape(row_count, -1).astype(half)
    block_rows = input_wide + jnp.dot(mixed_half, out_half, preferred_element_type=wide)
    block_out = block_rows.astype(half).reshape(seq_count, length, width)
    cotangent = out_grad.reshape(row_count, width)
    out_w_local = jnp.einsum("ti,td->id", mixed_half, cotangent, preferred_element_type=wide)
    d_mixed = jnp.einsum("td,id->ti", cotangent, out_half, preferred_element_type=wide)
    d_proj, grad_conv, grad_head, grad_gate = mixer_back(d_mixed.reshape(seq_count, length, -1))
    dproj_half = d_proj.reshape(row_count, -1).astype(half)
    main_cols = dproj_half.shape[1] // 128 * 128
    grad_main = jnp.einsum(
        "td,tk->dk", normed, dproj_half[:, :main_cols], preferred_element_type=wide
    )
    grad_tail = jnp.einsum(
        "td,tk->dk", normed, dproj_half[:, main_cols:], preferred_element_type=wide
    )
    d_normed = jnp.einsum("tk,dk->td", dproj_half, in_half, preferred_element_type=wide)
    norm_back = jax.vjp(norm_rows, input_wide, norm_wide)[1]
    d_input, grad_norm = norm_back(d_normed)
    input_grad = (cotangent.astype(wide) + d_input).reshape(seq_count, length, width)
    grp_size = 4
    own_rows = width // grp_size
    conv_cols = grad_conv.shape[1] // grp_size
    head_cols = grad_head.shape[1] // grp_size
    gate_size = grad_gate.shape[0] // grp_size
    small = [
        grad_norm.reshape(grp_size, -1),
        grad_gate.reshape(grp_size, -1),
        jnp.transpose(grad_conv.reshape(-1, grp_size, conv_cols), (1, 0, 2)).reshape(grp_size, -1),
        jnp.transpose(grad_head.reshape(-1, grp_size, head_cols), (1, 0, 2)).reshape(grp_size, -1),
    ]
    small = jnp.concatenate(small, axis=1)
    small_size = small.shape[1]
    tail_cols = grad_tail.shape[1]
    spare = 128 - tail_cols
    small = jnp.pad(small, ((0, 0), (0, own_rows * spare - small_size)))
    small = small.reshape(grp_size * own_rows, spare)
    grad_last = jnp.concatenate([grad_tail, small], axis=1)
    reduced = reduce_grads((grad_main, out_w_local, grad_last))
    groups = lax.axis_size("dp")
    step = 1 << BITS
    while step < groups:
        pairs = [(index, index ^ step) for index in range(groups)]
        reduced = [piece + lax.ppermute(piece, "dp", pairs) for piece in reduced]
        step *= 2
    main_sum, out_grad_w, last_sum = reduced
    flat = last_sum[:, tail_cols:].reshape(-1)
    norm_grad = flat[:own_rows]
    gate_grad = flat[own_rows : own_rows + gate_size]
    conv_at = own_rows + gate_size
    head_at = conv_at + grad_conv.shape[0] * conv_cols
    conv_grad = flat[conv_at:head_at].reshape(-1, conv_cols)
    head_grad = flat[head_at:small_size].reshape(-1, head_cols)
    local_squares = square_sum((main_sum, out_grad_w, last_sum))
    squares = lax.psum(local_squares, "grp")
    clip_factor = jnp.minimum(1.0, clip_limit / jnp.sqrt(squares + 1e-06))
    norm_new, norm_mom = adam_update(norm_gain, norm_gain_moments, norm_grad, clip_factor)
    in_grad, in_new, in_mom = update_weight(
        in_weight,
        in_weight_moments,
        (main_sum, last_sum),
        (main_cols, tail_cols),
        clip_factor,
        "update_in",
    )
    conv_new, conv_mom = adam_update(conv_params, conv_params_moments, conv_grad, clip_factor)
    head_new, head_mom = adam_update(head_params, head_params_moments, head_grad, clip_factor)
    gate_new, gate_mom = adam_update(gate_gain, gate_gain_moments, gate_grad, clip_factor)
    out_grad_w, out_new, out_mom = update_weight(
        out_weight, out_weight_moments, (out_grad_w,), (width,), clip_factor, "update_out"
    )
    return (
        block_out,
        input_grad,
        norm_grad,
        in_grad,
        conv_grad,
        head_grad,
        gate_grad,
        out_grad_w,
        norm_new,
        in_new,
        conv_new,
        head_new,
        gate_new,
        out_new,
        norm_mom,
        in_mom,
        conv_mom,
        head_mom,
        gate_mom,
        out_mom,
    )


def solution(mesh):
    in_specs = (
        P(("grp", "dp"), None, None),
        P(("grp", "dp"), None),
        P(("grp", "dp"), None, None),
        P("grp"),
        P("grp", None),
        P(None, "grp"),
        P(None, "grp"),
        P("grp"),
        P("grp", None),
        P(None, "grp"),
        P(None, "grp", None),
        P(None, None, "grp"),
        P(None, None, "grp"),
        P(None, "grp"),
        P(None, "grp", None),
    )
    out_specs = (
        P(("grp", "dp"), None, None),
        P(("grp", "dp"), None, None),
        P("grp"),
        P("grp", None),
        P(None, "grp"),
        P(None, "grp"),
        P("grp"),
        P("grp", None),
        P("grp"),
        P("grp", None),
        P(None, "grp"),
        P(None, "grp"),
        P("grp"),
        P("grp", None),
        P(None, "grp"),
        P(None, "grp", None),
        P(None, None, "grp"),
        P(None, None, "grp"),
        P(None, "grp"),
        P(None, "grp", None),
    )
    return jax.shard_map(shards, mesh=mesh, in_specs=in_specs, out_specs=out_specs, check_vma=False)
```
